32 devices in a mesh: space: 16 (over z, x, core), sample: 2 (over y).
Axes of the slice: x: 2, y: 2, z: 4, core: 2. Of those that a mesh axis runs over, the one named last changes fastest.
Arguments:
- spectra: float32 [36, 2, 512, 256], P('sample', None, 'space'), may hold values from -6 to 6
- plane_assign: int32 [2, 18], P('sample'), may hold values from 0 to 17, each once within a row
- fine_state: bfloat16 [4, 32, 131072], P('sample', 'space'), may hold values from 0.3984375 to 1.3984375
- partner_state: float32 [4, 4, 2048], P('sample'), may hold values from 0.4 to 1.4
- coarse_state: float32 [32, 4, 2048], P(('space', 'sample')), may hold values from 0.4 to 1.4
- turbine_x: int32 [16], replicated, may hold values from 0 to 31
- turbine_y: int32 [16], replicated, may hold values from 0 to 62
- turbine_z: int32 [16], replicated, may hold values from 0 to 30
- thrust: float32 [16], replicated, may hold values from 0.5 to 2
Outputs:
- fine_field: float32 [4, 32, 131072], P('sample', 'space')
- partner_field: float32 [4, 4, 2048], P('sample')
- coarse_field: float32 [32, 4, 2048], P(('space', 'sample'))
- estimate: float32 [2], replicated
The draws below stay inside these ranges and needn't reach their ends.
Inputs may be any that keep to these rules, and one draw needn't show every extreme that they name: `plane_assign`: each row is a permutation of 0 to 17.
All inputs are finite; a program needn't handle non-finite values.
Results may differ from the reference program's by a relative error of at most 0.0003.
Values sent between devices are 32-bit elements; how exact they have to be, the bound alone decides.
A program may use at most 128 MiB of HBM per device.

```python
import math
import jax
import jax.numpy as jnp
from jax import lax

NY = 512
NZ = 256
PAIRS_DEV = 2
COARSE_DEV = 1
STEPS = 2
NTURB = 16
NXF = 32
NXC = 4
NYC = 64
NZC = 32
GP = 18
PLANES = 36
PAIRS = 4
COARSE = 32
N_SPACE = 16
N_SAMPLE = 2


def set_ends(drawn, stream_key, least, largest):
    index_at = [jax.random.randint(jax.random.fold_in(stream_key, axis), (), 0, length) for axis, length in enumerate(drawn.shape)]
    longest = drawn.shape.index(max(drawn.shape))
    beside = index_at[:longest] + [(index_at[longest] + 1) % drawn.shape[longest]] + index_at[longest + 1:]
    return drawn.at[tuple(index_at)].set(least).at[tuple(beside)].set(largest)


def shard_levels(key, shape, shards, smallest, largest):
    def one(axis_at, parts):
        draws = jax.random.uniform(jax.random.fold_in(jax.random.fold_in(key, 6), axis_at), (parts,), jnp.float32, smallest / len(shards), largest / len(shards))
        return jnp.repeat(jnp.exp(draws), shape[axis_at] // parts).reshape((-1,) + (1,) * (len(shape) - axis_at - 1))

    level = one(*shards[0])
    for cut in shards[1:]:
        level = level * one(*cut)
    return level


def normal_values(rng, extent, width, most, cuts=(), kind=jnp.bfloat16):
    factor_of = shard_levels(rng, extent, cuts, -0.22, 0.18) if cuts else 1.0
    drawn = jax.random.normal(rng, extent, jnp.float32) * width * factor_of
    return jnp.minimum(jnp.maximum(drawn, -most), most).astype(kind)


def setup_inputs(seed: int = 0) -> dict:
    streams_of = jax.random.split(jax.random.key(seed), 10)
    spectra = normal_values(streams_of[0], (PLANES, 2, NY, NZ), 1.0, 6.0, ((0, 2), (2, 16)), jnp.float32)
    plane_assign = jax.vmap(lambda own: jax.random.permutation(own, GP))(jax.random.split(streams_of[1], N_SAMPLE)).reshape((N_SAMPLE, GP)).astype(jnp.int32)
    fine_state = jnp.clip(0.3984375 + 1.0 * jax.random.uniform(streams_of[2], (PAIRS, NXF, NY * NZ), jnp.float32) ** shard_levels(streams_of[2], (PAIRS, NXF, NY * NZ), ((0, 2), (1, 16)), -0.2, 0.2), 0.3984375, 1.3984375).astype(jnp.bfloat16)
    partner_state = jnp.clip(0.4 + 1 * jax.random.uniform(streams_of[3], (PAIRS, NXC, NYC * NZC), jnp.float32) ** shard_levels(streams_of[3], (PAIRS, NXC, NYC * NZC), ((0, 2),), -0.2, 0.2), 0.4, 1.4)
    coarse_state = jnp.clip(0.4 + 1 * jax.random.uniform(streams_of[4], (COARSE, NXC, NYC * NZC), jnp.float32) ** shard_levels(streams_of[4], (COARSE, NXC, NYC * NZC), ((0, 32),), -0.2, 0.2), 0.4, 1.4)
    turbine_x = set_ends(jax.random.randint(streams_of[5], (NTURB,), 0, NXF), jax.random.fold_in(streams_of[5], 1), 0, NXF - 1).astype(jnp.int32)
    turbine_y = set_ends(jax.random.randint(streams_of[6], (NTURB,), 0, NY // 8 - 1), jax.random.fold_in(streams_of[6], 1), 0, (NY // 8 - 1) - 1).astype(jnp.int32)
    turbine_z = set_ends(jax.random.randint(streams_of[7], (NTURB,), 0, NZ // 8 - 1), jax.random.fold_in(streams_of[7], 1), 0, (NZ // 8 - 1) - 1).astype(jnp.int32)
    thrust = jnp.clip(jax.random.uniform(streams_of[8], (NTURB,), jnp.float32, 0.5, 2.0), 0.5, 2.0)
    return {"spectra": spectra, "plane_assign": plane_assign, "fine_state": fine_state, "partner_state": partner_state, "coarse_state": coarse_state, "turbine_x": turbine_x, "turbine_y": turbine_y, "turbine_z": turbine_z, "thrust": thrust}


ADVECT = 0.3
DIFFUSE = 0.1
RELAX = 0.05
AMPLITUDE = 0.2
HIGHEST = lax.Precision.HIGHEST

def advance(extended, inflow, resistance):
    upstream = extended[..., :-2, :, :]
    centre = extended[..., 1:-1, :, :]
    downstream = extended[..., 2:, :, :]
    lateral = jnp.roll(centre, 1, -2) + jnp.roll(centre, -1, -2) + jnp.roll(centre, 1, -1) + jnp.roll(centre, -1, -1) - 4.0 * centre
    updated = centre + ADVECT * (upstream - centre) + DIFFUSE * (upstream + downstream - 2.0 * centre) + DIFFUSE * lateral + RELAX * (inflow[..., None, :, :] - centre)
    return updated / (1.0 + resistance)

def drag_field(turbine_x, turbine_y, turbine_z, thrust, first_plane, length, factor, y_count, z_count):
    block_size = 8 // factor
    planes = first_plane + jnp.arange(length, dtype=jnp.int32)
    along_x = jnp.where((turbine_x // factor)[:, None] == planes[None, :], thrust[:, None], jnp.zeros_like(thrust)[:, None])
    y_index = jnp.arange(y_count, dtype=jnp.int32)
    z_index = jnp.arange(z_count, dtype=jnp.int32)
    low_y = (turbine_y * block_size)[:, None]
    low_z = (turbine_z * block_size)[:, None]
    cover_y = ((y_index[None, :] >= low_y) & (y_index[None, :] < low_y + 2 * block_size)).astype(thrust.dtype)
    cover_z = ((z_index[None, :] >= low_z) & (z_index[None, :] < low_z + 2 * block_size)).astype(thrust.dtype)
    cross_mask = (cover_y[:, :, None] * cover_z[:, None, :]).reshape(thrust.shape[0], y_count * z_count)
    return jnp.dot(along_x.T, cross_mask, precision=HIGHEST).reshape(length, y_count, z_count)

def restrict(values):
    leading = values.shape[:-2]
    y_count = values.shape[-2]
    z_count = values.shape[-1]
    return values.reshape(leading + (y_count // 8, 8, z_count // 8, 8)).mean(axis=(-3, -1))

def run_whole(velocity, inflow, resistance):
    for step_index in range(STEPS):
        extended = jnp.concatenate([inflow[..., None, :, :], velocity, velocity[..., -1:, :, :]], axis=-3)
        velocity = advance(extended, inflow, resistance)
    return velocity

def noise_plane(spectrum):
    wave = jnp.fft.ifft2(spectrum[0] + 1j * spectrum[1])
    return (jnp.real(wave) * math.sqrt(NY * NZ)).astype(spectrum.dtype)

def reference(spectra, plane_assign, fine_state, partner_state, coarse_state, turbine_x, turbine_y, turbine_z, thrust):
    offsets = (jnp.arange(N_SAMPLE, dtype=jnp.int32) * GP)[:, None]
    pair_planes = (offsets + plane_assign[:, :PAIRS_DEV]).reshape(PAIRS).astype(jnp.int32)
    alone_rows = plane_assign[:, PAIRS_DEV:].reshape(N_SAMPLE, N_SPACE, COARSE_DEV)
    alone_planes = jnp.transpose(offsets[:, :, None] + alone_rows, (1, 0, 2)).reshape(COARSE).astype(jnp.int32)
    fine_drag = drag_field(turbine_x, turbine_y, turbine_z, thrust, 0, NXF, 1, NY, NZ)
    coarse_drag = drag_field(turbine_x, turbine_y, turbine_z, thrust, 0, NXC, 8, NYC, NZC)

    def one_pair(inputs):
        plane_index, state_fine, state_coarse = inputs
        plane_noise = noise_plane(spectra[plane_index])
        inflow = 1.0 + AMPLITUDE * plane_noise
        velocity = run_whole(state_fine.astype(jnp.float32).reshape(NXF, NY, NZ), inflow, fine_drag)
        fine_power = jnp.sum(fine_drag * velocity * velocity * velocity) / 256.0
        coarse_inflow = 1.0 + AMPLITUDE * restrict(plane_noise)
        partner = run_whole(state_coarse.reshape(NXC, NYC, NZC), coarse_inflow, coarse_drag)
        partner_power = jnp.sum(coarse_drag * partner * partner * partner) / 4.0
        return (velocity.reshape(NXF, NY * NZ), partner.reshape(NXC, NYC * NZC), fine_power - partner_power)

    def one_alone(inputs):
        plane_index, state_coarse = inputs
        inflow = 1.0 + AMPLITUDE * restrict(noise_plane(spectra[plane_index]))
        velocity = run_whole(state_coarse.reshape(NXC, NYC, NZC), inflow, coarse_drag)
        power = jnp.sum(coarse_drag * velocity * velocity * velocity) / 4.0
        return (velocity.reshape(NXC, NYC * NZC), power)
    fine_field, partner_field, differences = lax.map(one_pair, (pair_planes, fine_state, partner_state))
    coarse_field, powers = lax.map(one_alone, (alone_planes, coarse_state))
    estimate = jnp.stack([jnp.mean(differences), jnp.mean(powers)])
    return (fine_field, partner_field, coarse_field, estimate)
```

```python
import functools
import math

import jax
import jax.numpy as jnp
import ml_dtypes
import numpy as np
from jax import lax
from jax.experimental import pallas as pl
from jax.experimental.pallas import tpu as pltpu
from jax.sharding import PartitionSpec as P

AMPLITUDE = 0.2
HIGHEST = lax.Precision.HIGHEST
MESH = pl.DeviceIdType.MESH
F32 = jnp.float32
BF16 = jnp.bfloat16
NT = (((1,), (1,)), ((), ()))


def halves(table):
    high = table.astype(np.float32).astype(ml_dtypes.bfloat16)
    low = (table - high.astype(np.float64)).astype(np.float32).astype(ml_dtypes.bfloat16)
    return np.stack([high, low])


def tables(spaces, ky_rows, total_z):
    total_y = spaces * ky_rows
    z = np.arange(total_z)
    phase_z = 2 * np.pi / total_z * (np.outer(z, z) % total_z)
    cz, sz = np.cos(phase_z), np.sin(phase_z)
    z_table = np.block([[cz, sz], [-sz, cz]])
    y = np.arange(total_y)
    phase_y = 2 * np.pi / total_y * (np.outer(y, y) % total_y)
    cy, sy = np.cos(phase_y), np.sin(phase_y)
    order = y.reshape(spaces // 2, 2, ky_rows).transpose(1, 0, 2).reshape(-1)
    y_table = np.concatenate([cy[:, order], -sy[:, order]], axis=1)
    z_small = z_table.reshape(2 * total_z, 2, total_z // 8, 8).mean(-1).reshape(2 * total_z, -1)
    y_small = np.concatenate(
        [cy.reshape(total_y // 8, 8, total_y).mean(1), -sy.reshape(total_y // 8, 8, total_y).mean(1)]
    )
    return halves(z_table), halves(y_table), halves(z_small), halves(y_small)


def split(x):
    high = x.astype(BF16)
    return high, (x - high.astype(F32)).astype(BF16)


def dot(a, b):
    return jnp.dot(a, b, preferred_element_type=F32)


def dot_right(x, high, low):
    xh, xl = split(x)
    return dot(xh, high) + dot(xl, high) + dot(xh, low)


def dot_left(high, low, x):
    xh, xl = split(x)
    return dot(high, xh) + dot(high, xl) + dot(low, xh)


def kernel(
    spaces, samples, coarse_planes,
    fine_hbm, spec, assign, partner, coarse, turbines, thrust, zt_hbm, yt_hbm, z_small, y_small,
    rep, fine_out, partner_out, coarse_out, est_out,
    own, halo, block, gath, al_in, al_out, al_recv, zt, yt, pq_hi, pq_lo, g_ref, rk, kd, u1, part,
    parts, group, groups,
    halo_s, halo_r, own_sem, zt_sem, yt_sem, gx_s, gz_s, gc_s, g_r, gc_r, al_s, al_r, p_s, p_r,
    q_s, q_r,
):
    me = lax.axis_index("space")
    sample = lax.axis_index("sample")
    last = spaces - 1
    pairs, _, ny, nz = fine_hbm.shape
    ky = spec.shape[2]
    yc, width = coarse.shape[1], coarse.shape[2]
    zc = width // coarse_planes
    core = lax.rem(me, 2)
    chip = me // 2
    across = lax.rem(chip, 2)
    level = chip // 2
    levels = spaces // 4
    chip_x = chip + 1 - 2 * across
    dev_x = chip_x * 2 + core
    dev_c = me + 1 - 2 * core

    def remote(src, dst, send, recv, **where):
        return pltpu.make_async_remote_copy(
            src_ref=src, dst_ref=dst, send_sem=send, recv_sem=recv, device_id=where,
            device_id_type=MESH,
        )

    def others(count, mine, body):
        def step(i, carry):
            @pl.when(i != mine)
            def _():
                body(i)

            return carry

        lax.fori_loop(0, count, step, 0)

    barrier = pltpu.get_barrier_semaphore()
    others(spaces, me, lambda i: pl.semaphore_signal(
        barrier, inc=1, device_id={"space": i}, device_id_type=MESH))
    others(samples, sample, lambda i: pl.semaphore_signal(
        barrier, inc=1, device_id={"sample": i}, device_id_type=MESH))
    pl.semaphore_wait(barrier, spaces + samples - 2)

    def to_right(n, p):
        return remote(fine_hbm.at[n, p], halo.at[0, n, p], halo_s.at[0, n, p], halo_r.at[0, n, p],
                      space=jnp.minimum(me + 1, last))

    def to_left(n, p):
        return remote(fine_hbm.at[n, p], halo.at[1, n, p], halo_s.at[1, n, p], halo_r.at[1, n, p],
                      space=jnp.maximum(me - 1, 0))

    @pl.when(me < last)
    def _():
        for n in range(pairs):
            for p in (1, 0):
                to_right(n, p).start()

    @pl.when(me > 0)
    def _():
        for n in range(pairs):
            for p in (0, 1):
                to_left(n, p).start()

    zt_copy = pltpu.make_async_copy(zt_hbm, zt, zt_sem)
    yt_copy = pltpu.make_async_copy(yt_hbm, yt, yt_sem)
    own_copy = pltpu.make_async_copy(fine_hbm, own, own_sem)
    zt_copy.start()
    yt_copy.start()
    own_copy.start()

    for n in range(pairs):
        planes = spec[assign[0, n]]
        block[2 * n : 2 * n + 2] = planes
        gath[core, chip, 2 * n : 2 * n + 2] = planes

    def stage(p, carry):
        planes = spec[assign[0, pairs + p]]
        rows = pl.ds(pl.multiple_of(p * ky, ky), ky)
        al_in[rows, 0:nz] = planes[0]
        al_in[rows, nz : 2 * nz] = planes[1]
        return carry

    lax.fori_loop(0, spaces, stage, 0)

    send_x = remote(block, gath.at[core, chip], gx_s, g_r.at[chip], space=dev_x)
    send_x.start()

    def along(k, which, src, chip_of):
        return remote(src, gath.at[core, chip_of], gz_s.at[which, k], g_r.at[chip_of],
                      space=(k * 2 + across) * 2 + core)

    others(levels, level, lambda k: along(k, 0, block, chip).start())

    z_out = dot_right(al_in[...], z_small[0], z_small[1])
    al_out[...] = z_out.reshape(spaces, ky, 2 * zc)
    al_recv[me] = al_out[me]

    tx, ty, tz = turbines[0:1], turbines[1:2], turbines[2:3]
    count = tx.shape[1]

    def cover(index, low, size):
        return jnp.where((index >= low) & (index < low + 2 * size), 1.0, 0.0).astype(F32)

    cover_y = cover(lax.broadcasted_iota(jnp.int32, (ny, count), 0), ty * 8, 8)
    cover_z = cover(lax.broadcasted_iota(jnp.int32, (nz, count), 0), tz * 8, 8)

    for j in range(4):
        weight = jnp.where(tx == me * 2 + (j - 1), thrust[...], 0.0)
        drag = lax.dot_general(cover_y, cover_z * weight, NT, precision=HIGHEST,
                               preferred_element_type=F32)
        if j in (1, 2):
            kd[j - 1] = drag
        rk[j] = 1.0 / (1.0 + drag)

    def send_alone(p):
        return remote(al_out.at[p], al_recv.at[me], al_s.at[p], al_r.at[me], space=p)

    others(spaces, me, lambda p: send_alone(p).start())

    cell = lax.broadcasted_iota(jnp.int32, (width, count), 0)
    weight_c = jnp.where(tx // 8 == cell // zc, thrust[...], 0.0)
    cover_zc = cover(cell % zc, tz, 1)
    cover_yc = cover(lax.broadcasted_iota(jnp.int32, (yc, count), 0), ty, 1)
    kc = lax.dot_general(cover_yc, cover_zc * weight_c, NT, precision=HIGHEST,
                         preferred_element_type=F32)
    rkc = 1.0 / (1.0 + kc)

    def got(c):
        remote(block, gath.at[core, c], gx_s, g_r.at[c], space=dev_x).wait_recv()

    got(chip_x)
    others(levels, level, lambda k: along(k, 1, gath.at[core, chip_x], chip_x).start())
    others(levels, level, lambda k: got(k * 2 + across))
    others(levels, level, lambda k: got(k * 2 + 1 - across))
    send_c = remote(gath.at[core], gath.at[core], gc_s, gc_r, space=dev_c)
    send_c.start()

    others(spaces, me, lambda p: remote(
        al_out.at[p], al_recv.at[p], al_s.at[p], al_r.at[p], space=p).wait_recv())
    norm = 1.0 / math.sqrt(ny * nz)
    folded = dot_left(y_small[0], y_small[1], al_recv[...].reshape(spaces * ky, 2 * zc))
    alone = jnp.dot(folded[0:yc], rep[0], precision=HIGHEST, preferred_element_type=F32) + jnp.dot(
        folded[yc : 2 * yc], rep[1], precision=HIGHEST, preferred_element_type=F32)
    alone_g = 1.0 + (AMPLITUDE * norm) * alone

    lane = lax.broadcasted_iota(jnp.int32, (yc, width), 1)
    z_at = lane % zc

    def coarse_run(u, g):
        for _ in range(2):
            west = jnp.where(z_at == 0, pltpu.roll(u, width - zc + 1, 1), pltpu.roll(u, 1, 1))
            east = jnp.where(z_at == zc - 1, pltpu.roll(u, zc - 1, 1), pltpu.roll(u, width - 1, 1))
            up = jnp.where(lane < zc, g, pltpu.roll(u, zc, 1))
            down = jnp.where(lane >= width - zc, u, pltpu.roll(u, width - zc, 1))
            side = west + east + pltpu.roll(u, 1, 0) + pltpu.roll(u, yc - 1, 0)
            u = (0.05 * (u + g) + 0.4 * up + 0.1 * (down + side)) * rkc
        return u

    run = coarse_run(coarse[0], alone_g)
    coarse_out[0] = run
    alone_power = jnp.sum(kc * run * run * run) * 0.25

    zt_copy.wait()
    yt_copy.wait()
    send_c.wait_recv()
    rows = 128

    def z_stage(n, carry):
        real = gath[:, :, 2 * n].reshape(ny, nz)
        imag = gath[:, :, 2 * n + 1].reshape(ny, nz)
        pq = dot_right(jnp.concatenate([real, imag], axis=1), zt[0], zt[1])
        high, low = split(pq)
        for c in range(2):
            pq_hi[n, c * ny : (c + 1) * ny] = high[:, c * nz : (c + 1) * nz]
            pq_lo[n, c * ny : (c + 1) * ny] = low[:, c * nz : (c + 1) * nz]
        return carry

    lax.fori_loop(0, pairs, z_stage, 0)

    def y_stage(i, carry):
        n, r = i // (ny // rows), lax.rem(i, ny // rows)
        at = pl.ds(pl.multiple_of(r * rows, rows), rows)
        noise = (dot(yt[0, at], pq_hi[n]) + dot(yt[0, at], pq_lo[n]) + dot(yt[1, at], pq_hi[n]))
        g_ref[n, at] = 1.0 + (AMPLITUDE * norm) * noise
        return carry

    lax.fori_loop(0, pairs * (ny // rows), y_stage, 0)

    mean_z = jnp.where(
        lax.broadcasted_iota(jnp.int32, (nz, width), 0) // 8
        == lax.broadcasted_iota(jnp.int32, (nz, width), 1) % zc, 0.125, 0.0).astype(BF16)
    mean_y = jnp.where(
        lax.broadcasted_iota(jnp.int32, (yc, ny), 1) // 8
        == lax.broadcasted_iota(jnp.int32, (yc, ny), 0), 0.125, 0.0).astype(BF16)
    partner_power = 0.0
    for n in range(pairs):
        gh, gl = split(g_ref[n] - 1.0)
        th, tl = split(dot(gh, mean_z) + dot(gl, mean_z))
        partner_g = 1.0 + dot(mean_y, th) + dot(mean_y, tl)
        run = coarse_run(partner[n], partner_g)
        partner_out[n] = run
        partner_power += jnp.sum(kc * run * run * run) * 0.25

    own_copy.wait()

    def advance(c, w, e, g, r):
        side = pltpu.roll(c, 1, 0) + pltpu.roll(c, ny - 1, 0) + pltpu.roll(c, 1, 1) + pltpu.roll(
            c, nz - 1, 1)
        return (0.05 * (c + g) + 0.4 * w + 0.1 * (e + side)) * r

    def fine(n, power):
        g = g_ref[n]

        @pl.when(me > 0)
        def _():
            for p in (1, 0):
                to_right(n, p).wait_recv()
            u1[0] = advance(halo[0, n, 1], halo[0, n, 0], own[n, 0], g, rk[0])

        @pl.when(me == 0)
        def _():
            halo[0, n, 1] = g
            u1[0] = g

        @pl.when(me < last)
        def _():
            for p in (0, 1):
                to_left(n, p).wait_recv()
            u1[3] = advance(halo[1, n, 0], own[n, 1], halo[1, n, 1], g, rk[3])

        @pl.when(me == last)
        def _():
            halo[1, n, 0] = own[n, 1]

        u1[1] = advance(own[n, 0], halo[0, n, 1], own[n, 1], g, rk[1])
        u1[2] = advance(own[n, 1], own[n, 0], halo[1, n, 0], g, rk[2])

        @pl.when(me == last)
        def _():
            u1[3] = u1[2]

        for p in range(2):
            u = advance(u1[1 + p], u1[p], u1[2 + p], g, rk[1 + p])
            fine_out[n, p] = u
            power += jnp.sum(kd[p] * u * u * u)
        return power

    fine_power = lax.fori_loop(0, pairs, fine, jnp.float32(0.0)) * (1.0 / 256.0)
    leader = jnp.where(me == 0, 1.0, 0.0)
    lane8 = lax.broadcasted_iota(jnp.int32, (8, 128), 1)
    part[...] = jnp.where(lane8 == 0, fine_power - leader * partner_power,
                          jnp.where(lane8 == 1, alone_power, 0.0))
    parts[me] = part[...]

    def send_part(p):
        return remote(part, parts.at[me], p_s.at[p], p_r.at[me], space=p)

    others(spaces, me, lambda p: send_part(p).start())
    others(spaces, me, lambda p: remote(
        part, parts.at[p], p_s.at[p], p_r.at[p], space=p).wait_recv())
    group[...] = jnp.sum(parts[...], axis=0)
    groups[sample] = group[...]
    others(samples, sample, lambda p: remote(
        group, groups.at[sample], q_s.at[p], q_r.at[sample], sample=p).start())
    others(samples, sample, lambda p: remote(
        group, groups.at[p], q_s.at[p], q_r.at[p], sample=p).wait_recv())
    total = jnp.sum(groups[...], axis=0)
    est_out[...] = jnp.where(lane8 == 0, total * (1.0 / (pairs * samples)),
                             total * (1.0 / (spaces * samples)))

    @pl.when(me < last)
    def _():
        for n in range(pairs):
            for p in (1, 0):
                to_right(n, p).wait_send()

    @pl.when(me > 0)
    def _():
        for n in range(pairs):
            for p in (0, 1):
                to_left(n, p).wait_send()

    send_x.wait_send()
    others(levels, level, lambda k: along(k, 0, block, chip).wait_send())
    others(levels, level, lambda k: along(k, 1, gath.at[core, chip_x], chip_x).wait_send())
    send_c.wait_send()
    others(spaces, me, lambda p: send_alone(p).wait_send())
    others(spaces, me, lambda p: send_part(p).wait_send())
    others(samples, sample, lambda p: remote(
        group, groups.at[sample], q_s.at[p], q_r.at[sample], sample=p).wait_send())


def shards(
    spaces, samples, spectra, plane_assign, fine_state, partner_state, coarse_state,
    turbine_x, turbine_y, turbine_z, thrust,
):
    ky, nz = spectra.shape[2:]
    ny = ky * spaces
    pairs, slab = fine_state.shape[:2]
    planes = partner_state.shape[1]
    yc, zc = ny // 8, nz // 8
    width = planes * zc
    levels = spaces // 4
    zt, yt, zs, ys = tables(spaces, ky, nz)
    rep = np.zeros((2, 2 * zc, width), np.float32)
    for c in range(2):
        for x in range(planes):
            rep[c, c * zc + np.arange(zc), x * zc + np.arange(zc)] = 1.0

    def pack(state):
        return state.reshape(-1, planes, yc, zc).transpose(0, 2, 1, 3).reshape(-1, yc, width)

    def unpack(state):
        return state.reshape(-1, yc, planes, zc).transpose(0, 2, 1, 3).reshape(-1, planes, yc * zc)

    vmem = pl.BlockSpec(memory_space=pltpu.VMEM)
    anywhere = pl.BlockSpec(memory_space=pl.ANY)
    dma = pltpu.SemaphoreType.DMA
    field, partner, alone, est = pl.pallas_call(
        functools.partial(kernel, spaces, samples, planes),
        out_shape=(
            jax.ShapeDtypeStruct((pairs, slab, ny, nz), F32),
            jax.ShapeDtypeStruct((pairs, yc, width), F32),
            jax.ShapeDtypeStruct((1, yc, width), F32),
            jax.ShapeDtypeStruct((8, 128), F32),
        ),
        in_specs=[anywhere, vmem, pl.BlockSpec(memory_space=pltpu.SMEM), vmem, vmem, vmem, vmem,
                  anywhere, anywhere, vmem, vmem, vmem],
        out_specs=(vmem,) * 4,
        scratch_shapes=[
            pltpu.VMEM((pairs, 2, ny, nz), F32),
            pltpu.VMEM((2, pairs, 2, ny, nz), F32),
            pltpu.VMEM((2 * pairs, ky, nz), F32),
            pltpu.VMEM((2, spaces // 2, 2 * pairs, ky, nz), F32),
            pltpu.VMEM((spaces * ky, 2 * nz), F32),
            pltpu.VMEM((spaces, ky, 2 * zc), F32),
            pltpu.VMEM((spaces, ky, 2 * zc), F32),
            pltpu.VMEM(zt.shape, BF16),
            pltpu.VMEM(yt.shape, BF16),
            pltpu.VMEM((pairs, 2 * ny, nz), BF16),
            pltpu.VMEM((pairs, 2 * ny, nz), BF16),
            pltpu.VMEM((pairs, ny, nz), F32),
            pltpu.VMEM((4, ny, nz), F32),
            pltpu.VMEM((2, ny, nz), F32),
            pltpu.VMEM((4, ny, nz), F32),
            pltpu.VMEM((8, 128), F32),
            pltpu.VMEM((spaces, 8, 128), F32),
            pltpu.VMEM((8, 128), F32),
            pltpu.VMEM((samples, 8, 128), F32),
            dma((2, pairs, 2)), dma((2, pairs, 2)), dma, dma, dma,
            dma, dma((2, levels)), dma, dma((spaces // 2,)), dma,
            dma((spaces,)), dma((spaces,)), dma((spaces,)), dma((spaces,)),
            dma((samples,)), dma((samples,)),
        ],
        compiler_params=pltpu.CompilerParams(
            collective_id=0, has_side_effects=True, vmem_limit_bytes=60 * 1024 * 1024
        ),
    )(
        fine_state.astype(F32).reshape(pairs, slab, ny, nz),
        spectra, plane_assign, pack(partner_state), pack(coarse_state),
        jnp.stack([turbine_x, turbine_y, turbine_z]), thrust[None],
        jnp.asarray(zt), jnp.asarray(yt), jnp.asarray(zs), jnp.asarray(ys), jnp.asarray(rep),
    )
    return field.reshape(pairs, slab, ny * nz), unpack(partner), unpack(alone), est[0, :2]


def solution(mesh):
    return jax.shard_map(
        functools.partial(shards, mesh.shape["space"], mesh.shape["sample"]),
        mesh=mesh,
        in_specs=(
            P("sample", None, "space", None),
            P("sample", None),
            P("sample", "space", None),
            P("sample", None, None),
            P(("space", "sample"), None, None),
            P(),
            P(),
            P(),
            P(),
        ),
        out_specs=(
            P("sample", "space", None),
            P("sample", None, None),
            P(("space", "sample"), None, None),
            P(),
        ),
        check_vma=False,
    )
```

```python
import functools
import math

import jax
import jax.numpy as jnp
import ml_dtypes
import numpy as np
from jax import lax
from jax.experimental import pallas as pl
from jax.experimental.pallas import tpu as pltpu
from jax.sharding import PartitionSpec as P

AMPLITUDE = 0.2
HIGHEST = lax.Precision.HIGHEST
MESH = pl.DeviceIdType.MESH
F32 = jnp.float32
BF16 = jnp.bfloat16
NT = (((1,), (1,)), ((), ()))


def halves(table):
    high = table.astype(np.float32).astype(ml_dtypes.bfloat16)
    low = (table - high.astype(np.float64)).astype(np.float32).astype(ml_dtypes.bfloat16)
    return np.stack([high, low])


def tables(spaces, ky_rows, total_z):
    total_y = spaces * ky_rows
    z = np.arange(total_z)
    phase_z = 2 * np.pi / total_z * (np.outer(z, z) % total_z)
    cz, sz = np.cos(phase_z), np.sin(phase_z)
    z_table = np.block([[cz, sz], [-sz, cz]])
    y = np.arange(total_y)
    phase_y = 2 * np.pi / total_y * (np.outer(y, y) % total_y)
    cy, sy = np.cos(phase_y), np.sin(phase_y)
    order = y.reshape(spaces // 2, 2, ky_rows).transpose(1, 0, 2).reshape(-1)
    y_table = np.concatenate([cy[:, order], -sy[:, order]], axis=1)
    z_small = z_table.reshape(2 * total_z, 2, total_z // 8, 8).mean(-1).reshape(2 * total_z, -1)
    y_small = np.concatenate(
        [cy.reshape(total_y // 8, 8, total_y).mean(1), -sy.reshape(total_y // 8, 8, total_y).mean(1)]
    )
    return halves(z_table), halves(y_table), halves(z_small), halves(y_small)


def split(x):
    high = x.astype(BF16)
    return high, (x - high.astype(F32)).astype(BF16)


def dot(a, b):
    return jnp.dot(a, b, preferred_element_type=F32)


def dot_right(x, high, low):
    xh, xl = split(x)
    return dot(xh, high) + dot(xl, high) + dot(xh, low)


def dot_left(high, low, x):
    xh, xl = split(x)
    return dot(high, xh) + dot(high, xl) + dot(low, xh)


def kernel(
    spaces, samples,
    fine_hbm, spec, assign, partner, coarse, tx_ref, ty_ref, tz_ref, thrust, zt_hbm, yt_hbm, z_small, y_small,
    rep, fine_out, partner_out, coarse_out, est_out,
    own, halo, block, gath, al_in, al_out, al_recv, zt, yt, pq_hi, pq_lo, g_ref, rk, kd, u1, part,
    parts, group, groups,
    halo_s, halo_r, own_sem, zt_sem, yt_sem, gx_s, gz_s, gc_s, g_r, gc_r, al_s, al_r, p_s, p_r,
    q_s, q_r,
):
    me = lax.axis_index("space")
    sample = lax.axis_index("sample")
    last = spaces - 1
    pairs, _, ny, nz = fine_hbm.shape
    ky = spec.shape[2]
    yc, zc = ny // 8, nz // 8
    coarse_planes, cells = coarse.shape[1:]
    width = 128
    core = lax.rem(me, 2)
    chip = me // 2
    across = lax.rem(chip, 2)
    level = chip // 2
    levels = spaces // 4
    chip_x = chip + 1 - 2 * across
    dev_x = chip_x * 2 + core
    dev_c = me + 1 - 2 * core

    def remote(src, dst, send, recv, **where):
        return pltpu.make_async_remote_copy(
            src_ref=src, dst_ref=dst, send_sem=send, recv_sem=recv, device_id=where,
            device_id_type=MESH,
        )

    def others(count, mine, body):
        def step(i, carry):
            @pl.when(i != mine)
            def _():
                body(i)

            return carry

        lax.fori_loop(0, count, step, 0)

    barrier = pltpu.get_barrier_semaphore()
    others(spaces, me, lambda i: pl.semaphore_signal(
        barrier, inc=1, device_id={"space": i}, device_id_type=MESH))
    others(samples, sample, lambda i: pl.semaphore_signal(
        barrier, inc=1, device_id={"sample": i}, device_id_type=MESH))
    pl.semaphore_wait(barrier, spaces + samples - 2)

    def to_right(n, p):
        return remote(fine_hbm.at[n, p], halo.at[0, n, p], halo_s.at[0, n, p], halo_r.at[0, n, p],
                      space=jnp.minimum(me + 1, last))

    def to_left(n, p):
        return remote(fine_hbm.at[n, p], halo.at[1, n, p], halo_s.at[1, n, p], halo_r.at[1, n, p],
                      space=jnp.maximum(me - 1, 0))

    def start_halo(n):
        @pl.when(me < last)
        def _():
            for p in (1, 0):
                to_right(n, p).start()

        @pl.when(me > 0)
        def _():
            for p in (0, 1):
                to_left(n, p).start()

    zt_copy = pltpu.make_async_copy(zt_hbm, zt, zt_sem)
    yt_copy = pltpu.make_async_copy(yt_hbm, yt, yt_sem)
    own_copy = pltpu.make_async_copy(fine_hbm, own, own_sem)
    zt_copy.start()
    yt_copy.start()
    own_copy.start()

    for n in range(pairs):
        planes = spec[assign[0, n]]
        block[2 * n : 2 * n + 2] = planes
        gath[core, chip, 2 * n : 2 * n + 2] = planes

    def stage(p, carry):
        planes = spec[assign[0, pairs + p]]
        rows = pl.ds(pl.multiple_of(p * ky, ky), ky)
        al_in[rows, 0:nz] = planes[0]
        al_in[rows, nz : 2 * nz] = planes[1]
        return carry

    lax.fori_loop(0, spaces, stage, 0)

    send_x = remote(block, gath.at[core, chip], gx_s, g_r.at[chip], space=dev_x)
    send_x.start()

    def along(k, which, src, chip_of):
        return remote(src, gath.at[core, chip_of], gz_s.at[which, k], g_r.at[chip_of],
                      space=(k * 2 + across) * 2 + core)

    others(levels, level, lambda k: along(k, 0, block, chip).start())
    for n in range(pairs - 1):
        start_halo(n)

    z_out = dot_right(al_in[...], z_small[0], z_small[1])
    al_out[...] = z_out.reshape(spaces, ky, 2 * zc)
    al_recv[me] = al_out[me]

    def got(c):
        remote(block, gath.at[core, c], gx_s, g_r.at[c], space=dev_x).wait_recv()

    got(chip_x)
    others(levels, level, lambda k: along(k, 1, gath.at[core, chip_x], chip_x).start())

    def send_alone(p):
        return remote(al_out.at[p], al_recv.at[me], al_s.at[p], al_r.at[me], space=p)

    others(spaces, me, lambda p: send_alone(p).start())
    start_halo(pairs - 1)

    tx, ty, tz = tx_ref[...], ty_ref[...], tz_ref[...]
    count = tx.shape[1]

    def cover(index, low, size):
        return jnp.where((index >= low) & (index < low + 2 * size), 1.0, 0.0).astype(F32)

    cover_y = cover(lax.broadcasted_iota(jnp.int32, (ny, count), 0), ty * 8, 8)
    cover_z = cover(lax.broadcasted_iota(jnp.int32, (nz, count), 0), tz * 8, 8)

    for j in range(4):
        weight = jnp.where(tx == me * 2 + (j - 1), thrust[...], 0.0)
        drag = lax.dot_general(cover_y, cover_z * weight, NT, precision=HIGHEST,
                               preferred_element_type=F32)
        if j in (1, 2):
            kd[j - 1] = drag
        rk[j] = 1.0 / (1.0 + drag)

    cell = lax.broadcasted_iota(jnp.int32, (cells, count), 0)
    at_x = lax.broadcasted_iota(jnp.int32, (coarse_planes, count), 0)
    weight_c = jnp.where(tx // 8 == at_x, thrust[...], 0.0)
    cover_c = cover(cell // zc, ty, 1) * cover(cell % zc, tz, 1)
    kc = lax.dot_general(weight_c, cover_c, NT, precision=HIGHEST, preferred_element_type=F32)
    rkc = 1.0 / (1.0 + kc)

    others(levels, level, lambda k: got(k * 2 + across))
    others(levels, level, lambda k: got(k * 2 + 1 - across))
    send_c = remote(gath.at[core], gath.at[core], gc_s, gc_r, space=dev_c)
    send_c.start()

    others(spaces, me, lambda p: remote(
        al_out.at[p], al_recv.at[p], al_s.at[p], al_r.at[p], space=p).wait_recv())
    norm = 1.0 / math.sqrt(ny * nz)
    folded = dot_left(y_small[0], y_small[1], al_recv[...].reshape(spaces * ky, 2 * zc))
    alone = jnp.dot(folded[0:yc], rep[0], precision=HIGHEST, preferred_element_type=F32) + jnp.dot(
        folded[yc : 2 * yc], rep[1], precision=HIGHEST, preferred_element_type=F32)
    lane = lax.broadcasted_iota(jnp.int32, (yc, width), 1)
    row = lax.broadcasted_iota(jnp.int32, (yc, width), 0)
    repeats = width // zc
    fold = jnp.where(
        lax.broadcasted_iota(jnp.int32, (yc // repeats, yc), 1) // repeats
        == lax.broadcasted_iota(jnp.int32, (yc // repeats, yc), 0), 1.0, 0.0)

    def flat(full):
        kept = jnp.where(lane // zc == row % repeats, full, 0.0)
        tiles = jnp.dot(fold, kept, precision=HIGHEST, preferred_element_type=F32)
        return jnp.concatenate([tiles[j : j + 1] for j in range(yc // repeats)], axis=1)

    alone_g = 1.0 + (AMPLITUDE * norm) * flat(alone)
    z_at = lax.broadcasted_iota(jnp.int32, (coarse_planes, cells), 1) % zc

    def coarse_run(u, g):
        for _ in range(2):
            west = jnp.where(z_at == 0, pltpu.roll(u, cells - zc + 1, 1), pltpu.roll(u, 1, 1))
            east = jnp.where(z_at == zc - 1, pltpu.roll(u, zc - 1, 1), pltpu.roll(u, cells - 1, 1))
            up = jnp.concatenate([g, u[:-1]], axis=0)
            down = jnp.concatenate([u[1:], u[-1:]], axis=0)
            side = west + east + pltpu.roll(u, zc, 1) + pltpu.roll(u, cells - zc, 1)
            u = (0.05 * (u + g) + 0.4 * up + 0.1 * (down + side)) * rkc
        return u

    run = coarse_run(coarse[0], alone_g)
    coarse_out[0] = run
    alone_power = jnp.sum(kc * run * run * run) * 0.25

    zt_copy.wait()
    yt_copy.wait()
    send_c.wait_recv()
    rows = 128

    def z_stage(n, carry):
        real = gath[:, :, 2 * n].reshape(ny, nz)
        imag = gath[:, :, 2 * n + 1].reshape(ny, nz)
        pq = dot_right(jnp.concatenate([real, imag], axis=1), zt[0], zt[1])
        high, low = split(pq)
        for c in range(2):
            pq_hi[n, c * ny : (c + 1) * ny] = high[:, c * nz : (c + 1) * nz]
            pq_lo[n, c * ny : (c + 1) * ny] = low[:, c * nz : (c + 1) * nz]
        return carry

    lax.fori_loop(0, pairs, z_stage, 0)

    def y_stage(i, carry):
        n, r = i // (ny // rows), lax.rem(i, ny // rows)
        at = pl.ds(pl.multiple_of(r * rows, rows), rows)
        noise = (dot(yt[0, at], pq_hi[n]) + dot(yt[0, at], pq_lo[n]) + dot(yt[1, at], pq_hi[n]))
        g_ref[n, at] = 1.0 + (AMPLITUDE * norm) * noise
        return carry

    lax.fori_loop(0, pairs * (ny // rows), y_stage, 0)

    mean_z = jnp.where(
        lax.broadcasted_iota(jnp.int32, (nz, width), 0) // 8
        == lax.broadcasted_iota(jnp.int32, (nz, width), 1) % zc, 0.125, 0.0).astype(BF16)
    mean_y = jnp.where(
        lax.broadcasted_iota(jnp.int32, (yc, ny), 1) // 8
        == lax.broadcasted_iota(jnp.int32, (yc, ny), 0), 0.125, 0.0).astype(BF16)
    partner_power = 0.0
    for n in range(pairs):
        gh, gl = split(g_ref[n] - 1.0)
        th, tl = split(dot(gh, mean_z) + dot(gl, mean_z))
        partner_g = 1.0 + flat(dot(mean_y, th) + dot(mean_y, tl))
        run = coarse_run(partner[n], partner_g)
        partner_out[n] = run
        partner_power += jnp.sum(kc * run * run * run) * 0.25

    own_copy.wait()

    def advance(c, w, e, g, r):
        side = pltpu.roll(c, 1, 0) + pltpu.roll(c, ny - 1, 0) + pltpu.roll(c, 1, 1) + pltpu.roll(
            c, nz - 1, 1)
        return (0.05 * (c + g) + 0.4 * w + 0.1 * (e + side)) * r

    def fine(n, power):
        g = g_ref[n]

        @pl.when(me > 0)
        def _():
            for p in (1, 0):
                to_right(n, p).wait_recv()
            u1[0] = advance(halo[0, n, 1], halo[0, n, 0], own[n, 0], g, rk[0])

        @pl.when(me == 0)
        def _():
            halo[0, n, 1] = g
            u1[0] = g

        @pl.when(me < last)
        def _():
            for p in (0, 1):
                to_left(n, p).wait_recv()
            u1[3] = advance(halo[1, n, 0], own[n, 1], halo[1, n, 1], g, rk[3])

        @pl.when(me == last)
        def _():
            halo[1, n, 0] = own[n, 1]

        u1[1] = advance(own[n, 0], halo[0, n, 1], own[n, 1], g, rk[1])
        u1[2] = advance(own[n, 1], own[n, 0], halo[1, n, 0], g, rk[2])

        @pl.when(me == last)
        def _():
            u1[3] = u1[2]

        for p in range(2):
            u = advance(u1[1 + p], u1[p], u1[2 + p], g, rk[1 + p])
            fine_out[n, p] = u
            power += jnp.sum(kd[p] * u * u * u)
        return power

    fine_power = lax.fori_loop(0, pairs, fine, jnp.float32(0.0)) * (1.0 / 256.0)
    leader = jnp.where(me == 0, 1.0, 0.0)
    lane8 = lax.broadcasted_iota(jnp.int32, (8, 128), 1)
    part[...] = jnp.where(lane8 == 0, fine_power - leader * partner_power,
                          jnp.where(lane8 == 1, alone_power, 0.0))
    parts[me] = part[...]

    def send_part(p):
        return remote(part, parts.at[me], p_s.at[p], p_r.at[me], space=p)

    others(spaces, me, lambda p: send_part(p).start())
    others(spaces, me, lambda p: remote(
        part, parts.at[p], p_s.at[p], p_r.at[p], space=p).wait_recv())
    group[...] = jnp.sum(parts[...], axis=0)
    groups[sample] = group[...]
    others(samples, sample, lambda p: remote(
        group, groups.at[sample], q_s.at[p], q_r.at[sample], sample=p).start())
    others(samples, sample, lambda p: remote(
        group, groups.at[p], q_s.at[p], q_r.at[p], sample=p).wait_recv())
    total = jnp.sum(groups[...], axis=0)
    est_out[0] = jnp.sum(jnp.where(lane8 == 0, total, 0.0)) * (0.125 / (pairs * samples))
    est_out[1] = jnp.sum(jnp.where(lane8 == 1, total, 0.0)) * (0.125 / (spaces * samples))

    @pl.when(me < last)
    def _():
        for n in range(pairs):
            for p in (1, 0):
                to_right(n, p).wait_send()

    @pl.when(me > 0)
    def _():
        for n in range(pairs):
            for p in (0, 1):
                to_left(n, p).wait_send()

    send_x.wait_send()
    others(levels, level, lambda k: along(k, 0, block, chip).wait_send())
    others(levels, level, lambda k: along(k, 1, gath.at[core, chip_x], chip_x).wait_send())
    send_c.wait_send()
    others(spaces, me, lambda p: send_alone(p).wait_send())
    others(spaces, me, lambda p: send_part(p).wait_send())
    others(samples, sample, lambda p: remote(
        group, groups.at[sample], q_s.at[p], q_r.at[sample], sample=p).wait_send())


def shards(
    spaces, samples, spectra, plane_assign, fine_state, partner_state, coarse_state,
    turbine_x, turbine_y, turbine_z, thrust,
):
    ky, nz = spectra.shape[2:]
    ny = ky * spaces
    pairs, slab = fine_state.shape[:2]
    planes = partner_state.shape[1]
    yc, zc = ny // 8, nz // 8
    cells = yc * zc
    levels = spaces // 4
    zt, yt, zs, ys = tables(spaces, ky, nz)
    rep = np.zeros((2, 2 * zc, 128), np.float32)
    for c in range(2):
        for at in range(128):
            rep[c, c * zc + at % zc, at] = 1.0

    vmem = pl.BlockSpec(memory_space=pltpu.VMEM)
    anywhere = pl.BlockSpec(memory_space=pl.ANY)
    dma = pltpu.SemaphoreType.DMA
    field, partner, alone, est = pl.pallas_call(
        functools.partial(kernel, spaces, samples),
        out_shape=(
            jax.ShapeDtypeStruct((pairs, slab, ny, nz), F32),
            jax.ShapeDtypeStruct((pairs, planes, cells), F32),
            jax.ShapeDtypeStruct((1, planes, cells), F32),
            jax.ShapeDtypeStruct((2,), F32),
        ),
        in_specs=[anywhere, vmem, pl.BlockSpec(memory_space=pltpu.SMEM)] + [vmem] * 6 + [
                  anywhere, anywhere, vmem, vmem, vmem],
        out_specs=(vmem, vmem, vmem, pl.BlockSpec(memory_space=pltpu.SMEM)),
        scratch_shapes=[
            pltpu.VMEM((pairs, 2, ny, nz), F32),
            pltpu.VMEM((2, pairs, 2, ny, nz), F32),
            pltpu.VMEM((2 * pairs, ky, nz), F32),
            pltpu.VMEM((2, spaces // 2, 2 * pairs, ky, nz), F32),
            pltpu.VMEM((spaces * ky, 2 * nz), F32),
            pltpu.VMEM((spaces, ky, 2 * zc), F32),
            pltpu.VMEM((spaces, ky, 2 * zc), F32),
            pltpu.VMEM(zt.shape, BF16),
            pltpu.VMEM(yt.shape, BF16),
            pltpu.VMEM((pairs, 2 * ny, nz), BF16),
            pltpu.VMEM((pairs, 2 * ny, nz), BF16),
            pltpu.VMEM((pairs, ny, nz), F32),
            pltpu.VMEM((4, ny, nz), F32),
            pltpu.VMEM((2, ny, nz), F32),
            pltpu.VMEM((4, ny, nz), F32),
            pltpu.VMEM((8, 128), F32),
            pltpu.VMEM((spaces, 8, 128), F32),
            pltpu.VMEM((8, 128), F32),
            pltpu.VMEM((samples, 8, 128), F32),
            dma((2, pairs, 2)), dma((2, pairs, 2)), dma, dma, dma,
            dma, dma((2, levels)), dma, dma((spaces // 2,)), dma,
            dma((spaces,)), dma((spaces,)), dma((spaces,)), dma((spaces,)),
            dma((samples,)), dma((samples,)),
        ],
        compiler_params=pltpu.CompilerParams(
            collective_id=0, has_side_effects=True, vmem_limit_bytes=60 * 1024 * 1024
        ),
    )(
        fine_state.astype(F32).reshape(pairs, slab, ny, nz),
        spectra, plane_assign, partner_state, coarse_state,
        turbine_x[None], turbine_y[None], turbine_z[None], thrust[None],
        jnp.asarray(zt), jnp.asarray(yt), jnp.asarray(zs), jnp.asarray(ys), jnp.asarray(rep),
    )
    return field.reshape(pairs, slab, ny * nz), partner, alone, est


def solution(mesh):
    return jax.shard_map(
        functools.partial(shards, mesh.shape["space"], mesh.shape["sample"]),
        mesh=mesh,
        in_specs=(
            P("sample", None, "space", None),
            P("sample", None),
            P("sample", "space", None),
            P("sample", None, None),
            P(("space", "sample"), None, None),
            P(),
            P(),
            P(),
            P(),
        ),
        out_specs=(
            P("sample", "space", None),
            P("sample", None, None),
            P(("space", "sample"), None, None),
            P(),
        ),
        check_vma=False,
    )
```

```python
import functools
import math

import jax
import jax.numpy as jnp
import ml_dtypes
import numpy as np
from jax import lax
from jax.experimental import pallas as pl
from jax.experimental.pallas import tpu as pltpu
from jax.sharding import PartitionSpec as P

AMPLITUDE = 0.2
HIGHEST = lax.Precision.HIGHEST
MESH = pl.DeviceIdType.MESH
F32 = jnp.float32
BF16 = jnp.bfloat16
NT = (((1,), (1,)), ((), ()))


def halves(table):
    high = table.astype(np.float32).astype(ml_dtypes.bfloat16)
    low = (table - high.astype(np.float64)).astype(np.float32).astype(ml_dtypes.bfloat16)
    return np.stack([high, low])


def tables(spaces, ky_rows, total_z):
    total_y = spaces * ky_rows
    z = np.arange(total_z)
    phase_z = 2 * np.pi / total_z * (np.outer(z, z) % total_z)
    cz, sz = np.cos(phase_z), np.sin(phase_z)
    z_table = np.block([[cz, sz], [-sz, cz]])
    y = np.arange(total_y)
    phase_y = 2 * np.pi / total_y * (np.outer(y, y) % total_y)
    cy, sy = np.cos(phase_y), np.sin(phase_y)
    order = y.reshape(spaces // 2, 2, ky_rows).transpose(1, 0, 2).reshape(-1)
    y_table = np.concatenate([cy[:, order], -sy[:, order]], axis=1)
    z_small = z_table.reshape(2 * total_z, 2, total_z // 8, 8).mean(-1).reshape(2 * total_z, -1)
    y_small = np.concatenate(
        [cy.reshape(total_y // 8, 8, total_y).mean(1), -sy.reshape(total_y // 8, 8, total_y).mean(1)]
    )
    return halves(z_table), halves(y_table), halves(z_small), halves(y_small)


def split(x):
    high = x.astype(BF16)
    return high, (x - high.astype(F32)).astype(BF16)


def dot(a, b):
    return jnp.dot(a, b, preferred_element_type=F32)


def dot_right(x, high, low):
    xh, xl = split(x)
    return dot(xh, high) + dot(xl, high) + dot(xh, low)


def dot_left(high, low, x):
    xh, xl = split(x)
    return dot(high, xh) + dot(high, xl) + dot(low, xh)


def over(x, size):
    return lax.shift_right_logical(x, jnp.full_like(x, size.bit_length() - 1))


def within(x, size):
    return x & (size - 1)


def kernel(
    spaces, samples,
    fine_hbm, spec, assign, partner, coarse, tx_ref, ty_ref, tz_ref, thrust, zt_hbm, yt_hbm, z_small, y_small,
    rep, fine_out, partner_out, coarse_out, est_out,
    own, halo, block, gath, al_in, al_out, al_recv, zt, yt, pq_hi, pq_lo, g_ref, rk, kd, u1, part,
    parts, group, groups,
    halo_s, halo_r, own_sem, zt_sem, yt_sem, gx_s, gz_s, gc_s, g_r, gc_r, al_s, al_r, p_s, p_r,
    q_s, q_r,
):
    me = lax.axis_index("space")
    sample = lax.axis_index("sample")
    last = spaces - 1
    pairs, _, ny, nz = fine_hbm.shape
    ky = spec.shape[2]
    yc, zc = ny // 8, nz // 8
    coarse_planes, cells = coarse.shape[1:]
    width = 128
    core = lax.rem(me, 2)
    chip = me // 2
    across = lax.rem(chip, 2)
    level = chip // 2
    levels = spaces // 4
    chip_x = chip + 1 - 2 * across
    dev_x = chip_x * 2 + core
    dev_c = me + 1 - 2 * core

    def remote(src, dst, send, recv, **where):
        return pltpu.make_async_remote_copy(
            src_ref=src, dst_ref=dst, send_sem=send, recv_sem=recv, device_id=where,
            device_id_type=MESH,
        )

    def others(count, mine, body):
        def step(i, carry):
            @pl.when(i != mine)
            def _():
                body(i)

            return carry

        lax.fori_loop(0, count, step, 0)

    barrier = pltpu.get_barrier_semaphore()
    others(spaces, me, lambda i: pl.semaphore_signal(
        barrier, inc=1, device_id={"space": i}, device_id_type=MESH))
    others(samples, sample, lambda i: pl.semaphore_signal(
        barrier, inc=1, device_id={"sample": i}, device_id_type=MESH))
    pl.semaphore_wait(barrier, spaces + samples - 2)

    def to_right(n, p):
        return remote(fine_hbm.at[n, p], halo.at[0, n, p], halo_s.at[0, n, p], halo_r.at[0, n, p],
                      space=jnp.minimum(me + 1, last))

    def to_left(n, p):
        return remote(fine_hbm.at[n, p], halo.at[1, n, p], halo_s.at[1, n, p], halo_r.at[1, n, p],
                      space=jnp.maximum(me - 1, 0))

    def start_halo(n):
        @pl.when(me < last)
        def _():
            for p in (1, 0):
                to_right(n, p).start()

        @pl.when(me > 0)
        def _():
            for p in (0, 1):
                to_left(n, p).start()

    zt_copy = pltpu.make_async_copy(zt_hbm, zt, zt_sem)
    yt_copy = pltpu.make_async_copy(yt_hbm, yt, yt_sem)
    own_copy = pltpu.make_async_copy(fine_hbm, own, own_sem)
    zt_copy.start()
    yt_copy.start()
    own_copy.start()

    for n in range(pairs):
        planes = spec[assign[0, n]]
        block[2 * n : 2 * n + 2] = planes
        gath[core, chip, 2 * n : 2 * n + 2] = planes

    def stage(p, carry):
        planes = spec[assign[0, pairs + p]]
        rows = pl.ds(pl.multiple_of(p * ky, ky), ky)
        al_in[rows, 0:nz] = planes[0]
        al_in[rows, nz : 2 * nz] = planes[1]
        return carry

    lax.fori_loop(0, spaces, stage, 0)

    send_x = remote(block, gath.at[core, chip], gx_s, g_r.at[chip], space=dev_x)
    send_x.start()

    def along(k, which, src, chip_of):
        return remote(src, gath.at[core, chip_of], gz_s.at[which, k], g_r.at[chip_of],
                      space=(k * 2 + across) * 2 + core)

    others(levels, level, lambda k: along(k, 0, block, chip).start())
    for n in range(pairs - 1):
        start_halo(n)

    z_out = dot_right(al_in[...], z_small[0], z_small[1])
    al_out[...] = z_out.reshape(spaces, ky, 2 * zc)
    al_recv[me] = al_out[me]

    def got(c):
        remote(block, gath.at[core, c], gx_s, g_r.at[c], space=dev_x).wait_recv()

    got(chip_x)
    others(levels, level, lambda k: along(k, 1, gath.at[core, chip_x], chip_x).start())

    def send_alone(p):
        return remote(al_out.at[p], al_recv.at[me], al_s.at[p], al_r.at[me], space=p)

    others(spaces, me, lambda p: send_alone(p).start())
    start_halo(pairs - 1)

    tx, ty, tz = tx_ref[...], ty_ref[...], tz_ref[...]
    count = tx.shape[1]

    def cover(index, low, size):
        return jnp.where((index >= low) & (index < low + 2 * size), 1.0, 0.0).astype(F32)

    cover_y = cover(lax.broadcasted_iota(jnp.int32, (ny, count), 0), ty * 8, 8)
    cover_z = cover(lax.broadcasted_iota(jnp.int32, (nz, count), 0), tz * 8, 8)

    for j in range(4):
        weight = jnp.where(tx == me * 2 + (j - 1), thrust[...], 0.0)
        drag = lax.dot_general(cover_y, cover_z * weight, NT, precision=HIGHEST,
                               preferred_element_type=F32)
        if j in (1, 2):
            kd[j - 1] = drag
        rk[j] = 1.0 / (1.0 + drag)

    cell = lax.broadcasted_iota(jnp.int32, (cells, count), 0)
    at_x = lax.broadcasted_iota(jnp.int32, (coarse_planes, count), 0)
    weight_c = jnp.where(over(tx, 8) == at_x, thrust[...], 0.0)
    cover_c = cover(over(cell, zc), ty, 1) * cover(within(cell, zc), tz, 1)
    kc = lax.dot_general(weight_c, cover_c, NT, precision=HIGHEST, preferred_element_type=F32)
    rkc = 1.0 / (1.0 + kc)

    others(levels, level, lambda k: got(k * 2 + across))
    others(levels, level, lambda k: got(k * 2 + 1 - across))
    send_c = remote(gath.at[core], gath.at[core], gc_s, gc_r, space=dev_c)
    send_c.start()

    others(spaces, me, lambda p: remote(
        al_out.at[p], al_recv.at[p], al_s.at[p], al_r.at[p], space=p).wait_recv())
    norm = 1.0 / math.sqrt(ny * nz)
    folded = dot_left(y_small[0], y_small[1], al_recv[...].reshape(spaces * ky, 2 * zc))
    alone = jnp.dot(folded[0:yc], rep[0], precision=HIGHEST, preferred_element_type=F32) + jnp.dot(
        folded[yc : 2 * yc], rep[1], precision=HIGHEST, preferred_element_type=F32)
    lane = lax.broadcasted_iota(jnp.int32, (yc, width), 1)
    row = lax.broadcasted_iota(jnp.int32, (yc, width), 0)
    repeats = width // zc
    fold = jnp.where(
        over(lax.broadcasted_iota(jnp.int32, (yc // repeats, yc), 1), repeats)
        == lax.broadcasted_iota(jnp.int32, (yc // repeats, yc), 0), 1.0, 0.0)

    def flat(full):
        kept = jnp.where(over(lane, zc) == within(row, repeats), full, 0.0)
        tiles = jnp.dot(fold, kept, precision=HIGHEST, preferred_element_type=F32)
        return jnp.concatenate([tiles[j : j + 1] for j in range(yc // repeats)], axis=1)

    alone_g = 1.0 + (AMPLITUDE * norm) * flat(alone)
    z_at = within(lax.broadcasted_iota(jnp.int32, (coarse_planes, cells), 1), zc)

    def coarse_run(u, g):
        for _ in range(2):
            west = jnp.where(z_at == 0, pltpu.roll(u, cells - zc + 1, 1), pltpu.roll(u, 1, 1))
            east = jnp.where(z_at == zc - 1, pltpu.roll(u, zc - 1, 1), pltpu.roll(u, cells - 1, 1))
            up = jnp.concatenate([g, u[:-1]], axis=0)
            down = jnp.concatenate([u[1:], u[-1:]], axis=0)
            side = west + east + pltpu.roll(u, zc, 1) + pltpu.roll(u, cells - zc, 1)
            u = (0.05 * (u + g) + 0.4 * up + 0.1 * (down + side)) * rkc
        return u

    run = coarse_run(coarse[0], alone_g)
    coarse_out[0] = run
    alone_power = jnp.sum(kc * run * run * run) * 0.25

    zt_copy.wait()
    yt_copy.wait()
    send_c.wait_recv()
    rows = 128

    def z_stage(n, carry):
        real = gath[:, :, 2 * n].reshape(ny, nz)
        imag = gath[:, :, 2 * n + 1].reshape(ny, nz)
        pq = dot_right(jnp.concatenate([real, imag], axis=1), zt[0], zt[1])
        high, low = split(pq)
        for c in range(2):
            pq_hi[n, c * ny : (c + 1) * ny] = high[:, c * nz : (c + 1) * nz]
            pq_lo[n, c * ny : (c + 1) * ny] = low[:, c * nz : (c + 1) * nz]
        return carry

    lax.fori_loop(0, pairs, z_stage, 0)

    def y_stage(i, carry):
        n, r = i // (ny // rows), lax.rem(i, ny // rows)
        at = pl.ds(pl.multiple_of(r * rows, rows), rows)
        noise = (dot(yt[0, at], pq_hi[n]) + dot(yt[0, at], pq_lo[n]) + dot(yt[1, at], pq_hi[n]))
        g_ref[n, at] = 1.0 + (AMPLITUDE * norm) * noise
        return carry

    lax.fori_loop(0, pairs * (ny // rows), y_stage, 0)

    mean_z = jnp.where(
        over(lax.broadcasted_iota(jnp.int32, (nz, width), 0), 8)
        == within(lax.broadcasted_iota(jnp.int32, (nz, width), 1), zc), 0.125, 0.0).astype(BF16)
    mean_y = jnp.where(
        over(lax.broadcasted_iota(jnp.int32, (yc, ny), 1), 8)
        == lax.broadcasted_iota(jnp.int32, (yc, ny), 0), 0.125, 0.0).astype(BF16)
    partner_power = 0.0
    for n in range(pairs):
        gh, gl = split(g_ref[n] - 1.0)
        th, tl = split(dot(gh, mean_z) + dot(gl, mean_z))
        partner_g = 1.0 + flat(dot(mean_y, th) + dot(mean_y, tl))
        run = coarse_run(partner[n], partner_g)
        partner_out[n] = run
        partner_power += jnp.sum(kc * run * run * run) * 0.25

    own_copy.wait()

    def advance(c, w, e, g, r):
        side = pltpu.roll(c, 1, 0) + pltpu.roll(c, ny - 1, 0) + pltpu.roll(c, 1, 1) + pltpu.roll(
            c, nz - 1, 1)
        return (0.05 * (c + g) + 0.4 * w + 0.1 * (e + side)) * r

    def fine(n, power):
        g = g_ref[n]

        @pl.when(me > 0)
        def _():
            for p in (1, 0):
                to_right(n, p).wait_recv()
            u1[0] = advance(halo[0, n, 1], halo[0, n, 0], own[n, 0], g, rk[0])

        @pl.when(me == 0)
        def _():
            halo[0, n, 1] = g
            u1[0] = g

        @pl.when(me < last)
        def _():
            for p in (0, 1):
                to_left(n, p).wait_recv()
            u1[3] = advance(halo[1, n, 0], own[n, 1], halo[1, n, 1], g, rk[3])

        @pl.when(me == last)
        def _():
            halo[1, n, 0] = own[n, 1]

        u1[1] = advance(own[n, 0], halo[0, n, 1], own[n, 1], g, rk[1])
        u1[2] = advance(own[n, 1], own[n, 0], halo[1, n, 0], g, rk[2])

        @pl.when(me == last)
        def _():
            u1[3] = u1[2]

        for p in range(2):
            u = advance(u1[1 + p], u1[p], u1[2 + p], g, rk[1 + p])
            for h in range(nz // 128):
                fine_out[n, pl.ds(h * 2 + p, ny, stride=nz // 64), :] = u[:, h * 128 : h * 128 + 128]
            power += jnp.sum(kd[p] * u * u * u)
        return power

    fine_power = lax.fori_loop(0, pairs, fine, jnp.float32(0.0)) * (1.0 / 256.0)
    leader = jnp.where(me == 0, 1.0, 0.0)
    lane8 = lax.broadcasted_iota(jnp.int32, (8, 128), 1)
    part[...] = jnp.where(lane8 == 0, fine_power - leader * partner_power,
                          jnp.where(lane8 == 1, alone_power, 0.0))
    parts[me] = part[...]

    def send_part(p):
        return remote(part, parts.at[me], p_s.at[p], p_r.at[me], space=p)

    others(spaces, me, lambda p: send_part(p).start())
    others(spaces, me, lambda p: remote(
        part, parts.at[p], p_s.at[p], p_r.at[p], space=p).wait_recv())
    group[...] = jnp.sum(parts[...], axis=0)
    groups[sample] = group[...]
    others(samples, sample, lambda p: remote(
        group, groups.at[sample], q_s.at[p], q_r.at[sample], sample=p).start())
    others(samples, sample, lambda p: remote(
        group, groups.at[p], q_s.at[p], q_r.at[p], sample=p).wait_recv())
    total = jnp.sum(groups[...], axis=0)
    est_out[0] = jnp.sum(jnp.where(lane8 == 0, total, 0.0)) * (0.125 / (pairs * samples))
    est_out[1] = jnp.sum(jnp.where(lane8 == 1, total, 0.0)) * (0.125 / (spaces * samples))

    @pl.when(me < last)
    def _():
        for n in range(pairs):
            for p in (1, 0):
                to_right(n, p).wait_send()

    @pl.when(me > 0)
    def _():
        for n in range(pairs):
            for p in (0, 1):
                to_left(n, p).wait_send()

    send_x.wait_send()
    others(levels, level, lambda k: along(k, 0, block, chip).wait_send())
    others(levels, level, lambda k: along(k, 1, gath.at[core, chip_x], chip_x).wait_send())
    send_c.wait_send()
    others(spaces, me, lambda p: send_alone(p).wait_send())
    others(spaces, me, lambda p: send_part(p).wait_send())
    others(samples, sample, lambda p: remote(
        group, groups.at[sample], q_s.at[p], q_r.at[sample], sample=p).wait_send())


def shards(
    spaces, samples, spectra, plane_assign, fine_state, partner_state, coarse_state,
    turbine_x, turbine_y, turbine_z, thrust,
):
    ky, nz = spectra.shape[2:]
    ny = ky * spaces
    pairs, slab = fine_state.shape[:2]
    planes = partner_state.shape[1]
    yc, zc = ny // 8, nz // 8
    cells = yc * zc
    levels = spaces // 4
    zt, yt, zs, ys = tables(spaces, ky, nz)
    rep = np.zeros((2, 2 * zc, 128), np.float32)
    for c in range(2):
        for at in range(128):
            rep[c, c * zc + at % zc, at] = 1.0

    vmem = pl.BlockSpec(memory_space=pltpu.VMEM)
    anywhere = pl.BlockSpec(memory_space=pl.ANY)
    dma = pltpu.SemaphoreType.DMA
    field, partner, alone, est = pl.pallas_call(
        functools.partial(kernel, spaces, samples),
        out_shape=(
            jax.ShapeDtypeStruct((pairs, slab * ny * nz // 128, 128), F32),
            jax.ShapeDtypeStruct((pairs, planes, cells), F32),
            jax.ShapeDtypeStruct((1, planes, cells), F32),
            jax.ShapeDtypeStruct((2,), F32),
        ),
        in_specs=[anywhere, vmem, pl.BlockSpec(memory_space=pltpu.SMEM)] + [vmem] * 6 + [
                  anywhere, anywhere, vmem, vmem, vmem],
        out_specs=(vmem, vmem, vmem, pl.BlockSpec(memory_space=pltpu.SMEM)),
        scratch_shapes=[
            pltpu.VMEM((pairs, 2, ny, nz), F32),
            pltpu.VMEM((2, pairs, 2, ny, nz), F32),
            pltpu.VMEM((2 * pairs, ky, nz), F32),
            pltpu.VMEM((2, spaces // 2, 2 * pairs, ky, nz), F32),
            pltpu.VMEM((spaces * ky, 2 * nz), F32),
            pltpu.VMEM((spaces, ky, 2 * zc), F32),
            pltpu.VMEM((spaces, ky, 2 * zc), F32),
            pltpu.VMEM(zt.shape, BF16),
            pltpu.VMEM(yt.shape, BF16),
            pltpu.VMEM((pairs, 2 * ny, nz), BF16),
            pltpu.VMEM((pairs, 2 * ny, nz), BF16),
            pltpu.VMEM((pairs, ny, nz), F32),
            pltpu.VMEM((4, ny, nz), F32),
            pltpu.VMEM((2, ny, nz), F32),
            pltpu.VMEM((4, ny, nz), F32),
            pltpu.VMEM((8, 128), F32),
            pltpu.VMEM((spaces, 8, 128), F32),
            pltpu.VMEM((8, 128), F32),
            pltpu.VMEM((samples, 8, 128), F32),
            dma((2, pairs, 2)), dma((2, pairs, 2)), dma, dma, dma,
            dma, dma((2, levels)), dma, dma((spaces // 2,)), dma,
            dma((spaces,)), dma((spaces,)), dma((spaces,)), dma((spaces,)),
            dma((samples,)), dma((samples,)),
        ],
        compiler_params=pltpu.CompilerParams(
            collective_id=0, has_side_effects=True, vmem_limit_bytes=60 * 1024 * 1024
        ),
    )(
        fine_state.astype(F32).reshape(pairs, slab, ny, nz),
        spectra, plane_assign, partner_state, coarse_state,
        turbine_x[None], turbine_y[None], turbine_z[None], thrust[None],
        jnp.asarray(zt), jnp.asarray(yt), jnp.asarray(zs), jnp.asarray(ys), jnp.asarray(rep),
    )
    field = field.reshape(pairs, ny * nz // 128, slab, 128).transpose(0, 2, 1, 3)
    return field.reshape(pairs, slab, ny * nz), partner, alone, est


def solution(mesh):
    return jax.shard_map(
        functools.partial(shards, mesh.shape["space"], mesh.shape["sample"]),
        mesh=mesh,
        in_specs=(
            P("sample", None, "space", None),
            P("sample", None),
            P("sample", "space", None),
            P("sample", None, None),
            P(("space", "sample"), None, None),
            P(),
            P(),
            P(),
            P(),
        ),
        out_specs=(
            P("sample", "space", None),
            P("sample", None, None),
            P(("space", "sample"), None, None),
            P(),
        ),
        check_vma=False,
    )
```

```python
import functools
import math

import jax
import jax.numpy as jnp
import ml_dtypes
import numpy as np
from jax import lax
from jax.experimental import pallas as pl
from jax.experimental.pallas import tpu as pltpu
from jax.sharding import PartitionSpec as P

AMPLITUDE = 0.2
HIGHEST = lax.Precision.HIGHEST
MESH = pl.DeviceIdType.MESH
F32 = jnp.float32
BF16 = jnp.bfloat16
NT = (((1,), (1,)), ((), ()))


def halves(table):
    high = table.astype(np.float32).astype(ml_dtypes.bfloat16)
    low = (table - high.astype(np.float64)).astype(np.float32).astype(ml_dtypes.bfloat16)
    return np.stack([high, low])


def tables(spaces, ky_rows, total_z):
    total_y = spaces * ky_rows
    z = np.arange(total_z)
    phase_z = 2 * np.pi / total_z * (np.outer(z, z) % total_z)
    cz, sz = np.cos(phase_z), np.sin(phase_z)
    z_table = np.block([[cz, sz], [-sz, cz]])
    y = np.arange(total_y)
    phase_y = 2 * np.pi / total_y * (np.outer(y, y) % total_y)
    cy, sy = np.cos(phase_y), np.sin(phase_y)
    order = y.reshape(spaces // 2, 2, ky_rows).transpose(1, 0, 2).reshape(-1)
    y_table = np.concatenate([cy[:, order], -sy[:, order]], axis=1)
    z_small = z_table.reshape(2 * total_z, 2, total_z // 8, 8).mean(-1).reshape(2 * total_z, -1)
    y_small = np.concatenate(
        [cy.reshape(total_y // 8, 8, total_y).mean(1), -sy.reshape(total_y // 8, 8, total_y).mean(1)]
    )
    return halves(z_table), halves(y_table), halves(z_small), halves(y_small)


def split(x):
    high = x.astype(BF16)
    return high, (x - high.astype(F32)).astype(BF16)


def dot(a, b):
    return jnp.dot(a, b, preferred_element_type=F32)


def dot_right(x, high, low):
    xh, xl = split(x)
    return dot(xh, high) + dot(xl, high) + dot(xh, low)


def dot_left(high, low, x):
    xh, xl = split(x)
    return dot(high, xh) + dot(high, xl) + dot(low, xh)


def over(x, size):
    return lax.shift_right_logical(x, jnp.full_like(x, size.bit_length() - 1))


def within(x, size):
    return x & (size - 1)


def kernel(
    spaces, samples,
    fine_hbm, spec, assign, partner, coarse, tx_ref, ty_ref, tz_ref, thrust, zt_hbm, yt_hbm, z_small, y_small,
    rep, fine_out, partner_out, coarse_out, est_out,
    own, halo, block, gath, al_in, al_out, al_recv, zt, yt, pq_hi, pq_lo, g_ref, rk, kd, u1, part,
    parts, group, groups,
    halo_s, halo_r, own_sem, zt_sem, yt_sem, gx_s, gz_s, gc_s, g_r, gc_r, al_s, al_r, p_s, p_r,
    q_s, q_r,
):
    me = lax.axis_index("space")
    sample = lax.axis_index("sample")
    last = spaces - 1
    pairs, _, ny, nz = fine_hbm.shape
    ky = spec.shape[2]
    yc, zc = ny // 8, nz // 8
    coarse_planes, cells = coarse.shape[1:]
    width = 128
    core = lax.rem(me, 2)
    chip = me // 2
    across = lax.rem(chip, 2)
    level = chip // 2
    levels = spaces // 4
    chip_x = chip + 1 - 2 * across
    dev_x = chip_x * 2 + core
    dev_c = me + 1 - 2 * core

    def remote(src, dst, send, recv, **where):
        return pltpu.make_async_remote_copy(
            src_ref=src, dst_ref=dst, send_sem=send, recv_sem=recv, device_id=where,
            device_id_type=MESH,
        )

    def others(count, mine, body):
        def step(i, carry):
            @pl.when(i != mine)
            def _():
                body(i)

            return carry

        lax.fori_loop(0, count, step, 0)

    barrier = pltpu.get_barrier_semaphore()
    others(spaces, me, lambda i: pl.semaphore_signal(
        barrier, inc=1, device_id={"space": i}, device_id_type=MESH))
    others(samples, sample, lambda i: pl.semaphore_signal(
        barrier, inc=1, device_id={"sample": i}, device_id_type=MESH))
    for n in range(pairs):
        planes = spec[assign[0, n]]
        block[2 * n : 2 * n + 2] = planes
        gath[core, chip, 2 * n : 2 * n + 2] = planes
    pl.semaphore_wait(barrier, spaces + samples - 2)

    def to_right(n, p):
        return remote(fine_hbm.at[n, p], halo.at[0, n, p], halo_s.at[0, n, p], halo_r.at[0, n, p],
                      space=jnp.minimum(me + 1, last))

    def to_left(n, p):
        return remote(fine_hbm.at[n, p], halo.at[1, n, p], halo_s.at[1, n, p], halo_r.at[1, n, p],
                      space=jnp.maximum(me - 1, 0))

    def start_halo(n):
        @pl.when(me < last)
        def _():
            for p in (1, 0):
                to_right(n, p).start()

        @pl.when(me > 0)
        def _():
            for p in (0, 1):
                to_left(n, p).start()

    send_x = remote(block, gath.at[core, chip], gx_s, g_r.at[chip], space=dev_x)
    send_x.start()

    def along(k, which, src, chip_of):
        return remote(src, gath.at[core, chip_of], gz_s.at[which, k], g_r.at[chip_of],
                      space=(k * 2 + across) * 2 + core)

    others(levels, level, lambda k: along(k, 0, block, chip).start())
    for n in range(pairs - 1):
        start_halo(n)

    zt_copy = pltpu.make_async_copy(zt_hbm, zt, zt_sem)
    yt_copy = pltpu.make_async_copy(yt_hbm, yt, yt_sem)
    own_copy = pltpu.make_async_copy(fine_hbm, own, own_sem)
    zt_copy.start()
    yt_copy.start()
    own_copy.start()

    def stage(p, carry):
        planes = spec[assign[0, pairs + p]]
        rows = pl.ds(pl.multiple_of(p * ky, ky), ky)
        al_in[rows, 0:nz] = planes[0]
        al_in[rows, nz : 2 * nz] = planes[1]
        return carry

    lax.fori_loop(0, spaces, stage, 0)

    z_out = dot_right(al_in[...], z_small[0], z_small[1])
    z_out = z_out.reshape(spaces, ky, 2 * zc)
    al_out[...] = jnp.concatenate([z_out[:, : ky // 2], z_out[:, ky // 2 :]], axis=2)
    al_recv[me] = al_out[me]

    def got(c):
        remote(block, gath.at[core, c], gx_s, g_r.at[c], space=dev_x).wait_recv()

    got(chip_x)
    others(levels, level, lambda k: along(k, 1, gath.at[core, chip_x], chip_x).start())

    def send_alone(p):
        return remote(al_out.at[p], al_recv.at[me], al_s.at[p], al_r.at[me], space=p)

    others(spaces, me, lambda p: send_alone(p).start())
    start_halo(pairs - 1)

    tx, ty, tz = tx_ref[...], ty_ref[...], tz_ref[...]
    count = tx.shape[1]

    def cover(index, low, size):
        return jnp.where((index >= low) & (index < low + 2 * size), 1.0, 0.0).astype(F32)

    cover_y = cover(lax.broadcasted_iota(jnp.int32, (ny, count), 0), ty * 8, 8)
    cover_z = cover(lax.broadcasted_iota(jnp.int32, (nz, count), 0), tz * 8, 8)

    for j in range(4):
        weight = jnp.where(tx == me * 2 + (j - 1), thrust[...], 0.0)
        drag = lax.dot_general(cover_y, cover_z * weight, NT, precision=HIGHEST,
                               preferred_element_type=F32)
        if j in (1, 2):
            kd[j - 1] = drag
        rk[j] = 1.0 / (1.0 + drag)

    cell = lax.broadcasted_iota(jnp.int32, (cells, count), 0)
    at_x = lax.broadcasted_iota(jnp.int32, (coarse_planes, count), 0)
    weight_c = jnp.where(over(tx, 8) == at_x, thrust[...], 0.0)
    cover_c = cover(over(cell, zc), ty, 1) * cover(within(cell, zc), tz, 1)
    kc = lax.dot_general(weight_c, cover_c, NT, precision=HIGHEST, preferred_element_type=F32)
    rkc = 1.0 / (1.0 + kc)

    others(levels, level, lambda k: got(k * 2 + across))
    others(levels, level, lambda k: got(k * 2 + 1 - across))
    send_c = remote(gath.at[core], gath.at[core], gc_s, gc_r, space=dev_c)
    send_c.start()

    others(spaces, me, lambda p: remote(
        al_out.at[p], al_recv.at[p], al_s.at[p], al_r.at[p], space=p).wait_recv())
    norm = 1.0 / math.sqrt(ny * nz)
    packed = al_recv[...]
    packed = jnp.concatenate([packed[:, :, : 2 * zc], packed[:, :, 2 * zc :]], axis=1)
    folded = dot_left(y_small[0], y_small[1], packed.reshape(spaces * ky, 2 * zc))
    alone = jnp.dot(folded[0:yc], rep[0], precision=HIGHEST, preferred_element_type=F32) + jnp.dot(
        folded[yc : 2 * yc], rep[1], precision=HIGHEST, preferred_element_type=F32)
    lane = lax.broadcasted_iota(jnp.int32, (yc, width), 1)
    row = lax.broadcasted_iota(jnp.int32, (yc, width), 0)
    repeats = width // zc
    fold = jnp.where(
        over(lax.broadcasted_iota(jnp.int32, (yc // repeats, yc), 1), repeats)
        == lax.broadcasted_iota(jnp.int32, (yc // repeats, yc), 0), 1.0, 0.0)

    def flat(full):
        kept = jnp.where(over(lane, zc) == within(row, repeats), full, 0.0)
        tiles = jnp.dot(fold, kept, precision=HIGHEST, preferred_element_type=F32)
        return jnp.concatenate([tiles[j : j + 1] for j in range(yc // repeats)], axis=1)

    alone_g = 1.0 + (AMPLITUDE * norm) * flat(alone)
    z_at = within(lax.broadcasted_iota(jnp.int32, (coarse_planes, cells), 1), zc)

    def coarse_run(u, g):
        for _ in range(2):
            west = jnp.where(z_at == 0, pltpu.roll(u, cells - zc + 1, 1), pltpu.roll(u, 1, 1))
            east = jnp.where(z_at == zc - 1, pltpu.roll(u, zc - 1, 1), pltpu.roll(u, cells - 1, 1))
            up = jnp.concatenate([g, u[:-1]], axis=0)
            down = jnp.concatenate([u[1:], u[-1:]], axis=0)
            side = west + east + pltpu.roll(u, zc, 1) + pltpu.roll(u, cells - zc, 1)
            u = (0.05 * (u + g) + 0.4 * up + 0.1 * (down + side)) * rkc
        return u

    run = coarse_run(coarse[0], alone_g)
    coarse_out[0] = run
    alone_power = jnp.sum(kc * run * run * run) * 0.25

    zt_copy.wait()
    yt_copy.wait()
    send_c.wait_recv()
    rows = 128

    def z_stage(n, carry):
        real = gath[:, :, 2 * n].reshape(ny, nz)
        imag = gath[:, :, 2 * n + 1].reshape(ny, nz)
        pq = dot_right(jnp.concatenate([real, imag], axis=1), zt[0], zt[1])
        high, low = split(pq)
        for c in range(2):
            pq_hi[n, c * ny : (c + 1) * ny] = high[:, c * nz : (c + 1) * nz]
            pq_lo[n, c * ny : (c + 1) * ny] = low[:, c * nz : (c + 1) * nz]
        return carry

    lax.fori_loop(0, pairs, z_stage, 0)

    def y_stage(i, carry):
        n, r = i // (ny // rows), lax.rem(i, ny // rows)
        at = pl.ds(pl.multiple_of(r * rows, rows), rows)
        noise = (dot(yt[0, at], pq_hi[n]) + dot(yt[0, at], pq_lo[n]) + dot(yt[1, at], pq_hi[n]))
        g_ref[n, at] = 1.0 + (AMPLITUDE * norm) * noise
        return carry

    lax.fori_loop(0, pairs * (ny // rows), y_stage, 0)

    mean_z = jnp.where(
        over(lax.broadcasted_iota(jnp.int32, (nz, width), 0), 8)
        == within(lax.broadcasted_iota(jnp.int32, (nz, width), 1), zc), 0.125, 0.0).astype(BF16)
    mean_y = jnp.where(
        over(lax.broadcasted_iota(jnp.int32, (yc, ny), 1), 8)
        == lax.broadcasted_iota(jnp.int32, (yc, ny), 0), 0.125, 0.0).astype(BF16)
    partner_power = 0.0
    for n in range(pairs):
        gh, gl = split(g_ref[n] - 1.0)
        th, tl = split(dot(gh, mean_z) + dot(gl, mean_z))
        partner_g = 1.0 + flat(dot(mean_y, th) + dot(mean_y, tl))
        run = coarse_run(partner[n], partner_g)
        partner_out[n] = run
        partner_power += jnp.sum(kc * run * run * run) * 0.25

    own_copy.wait()

    def advance(c, w, e, g, r):
        side = pltpu.roll(c, 1, 0) + pltpu.roll(c, ny - 1, 0) + pltpu.roll(c, 1, 1) + pltpu.roll(
            c, nz - 1, 1)
        return (0.05 * (c + g) + 0.4 * w + 0.1 * (e + side)) * r

    def fine(n, power):
        g = g_ref[n]

        @pl.when(me > 0)
        def _():
            to_right(n, 1).wait_recv()

        @pl.when(me == 0)
        def _():
            halo[0, n, 1] = g

        @pl.when(me < last)
        def _():
            to_left(n, 0).wait_recv()

        @pl.when(me == last)
        def _():
            halo[1, n, 0] = own[n, 1]

        u1[1] = advance(own[n, 0], halo[0, n, 1], own[n, 1], g, rk[1])
        u1[2] = advance(own[n, 1], own[n, 0], halo[1, n, 0], g, rk[2])

        @pl.when(me > 0)
        def _():
            to_right(n, 0).wait_recv()
            u1[0] = advance(halo[0, n, 1], halo[0, n, 0], own[n, 0], g, rk[0])

        @pl.when(me == 0)
        def _():
            u1[0] = g

        @pl.when(me < last)
        def _():
            to_left(n, 1).wait_recv()
            u1[3] = advance(halo[1, n, 0], own[n, 1], halo[1, n, 1], g, rk[3])

        @pl.when(me == last)
        def _():
            u1[3] = u1[2]

        for p in range(2):
            u = advance(u1[1 + p], u1[p], u1[2 + p], g, rk[1 + p])
            for h in range(nz // 128):
                fine_out[n, pl.ds(h * 2 + p, ny, stride=nz // 64), :] = u[:, h * 128 : h * 128 + 128]
            power += jnp.sum(kd[p] * u * u * u)
        return power

    fine_power = lax.fori_loop(0, pairs, fine, jnp.float32(0.0)) * (1.0 / 256.0)
    leader = jnp.where(me == 0, 1.0, 0.0)
    lane8 = lax.broadcasted_iota(jnp.int32, (8, 128), 1)
    part[...] = jnp.where(lane8 == 0, fine_power - leader * partner_power,
                          jnp.where(lane8 == 1, alone_power, 0.0))
    parts[me] = part[...]

    def send_part(p):
        return remote(part, parts.at[me], p_s.at[p], p_r.at[me], space=p)

    others(spaces, me, lambda p: send_part(p).start())
    others(spaces, me, lambda p: remote(
        part, parts.at[p], p_s.at[p], p_r.at[p], space=p).wait_recv())
    group[...] = jnp.sum(parts[...], axis=0)
    groups[sample] = group[...]
    others(samples, sample, lambda p: remote(
        group, groups.at[sample], q_s.at[p], q_r.at[sample], sample=p).start())
    others(samples, sample, lambda p: remote(
        group, groups.at[p], q_s.at[p], q_r.at[p], sample=p).wait_recv())
    total = jnp.sum(groups[...], axis=0)
    est_out[0] = jnp.sum(jnp.where(lane8 == 0, total, 0.0)) * (0.125 / (pairs * samples))
    est_out[1] = jnp.sum(jnp.where(lane8 == 1, total, 0.0)) * (0.125 / (spaces * samples))

    @pl.when(me < last)
    def _():
        for n in range(pairs):
            for p in (1, 0):
                to_right(n, p).wait_send()

    @pl.when(me > 0)
    def _():
        for n in range(pairs):
            for p in (0, 1):
                to_left(n, p).wait_send()

    send_x.wait_send()
    others(levels, level, lambda k: along(k, 0, block, chip).wait_send())
    others(levels, level, lambda k: along(k, 1, gath.at[core, chip_x], chip_x).wait_send())
    send_c.wait_send()
    others(spaces, me, lambda p: send_alone(p).wait_send())
    others(spaces, me, lambda p: send_part(p).wait_send())
    others(samples, sample, lambda p: remote(
        group, groups.at[sample], q_s.at[p], q_r.at[sample], sample=p).wait_send())


def shards(
    spaces, samples, spectra, plane_assign, fine_state, partner_state, coarse_state,
    turbine_x, turbine_y, turbine_z, thrust,
):
    ky, nz = spectra.shape[2:]
    ny = ky * spaces
    pairs, slab = fine_state.shape[:2]
    planes = partner_state.shape[1]
    yc, zc = ny // 8, nz // 8
    cells = yc * zc
    levels = spaces // 4
    zt, yt, zs, ys = tables(spaces, ky, nz)
    rep = np.zeros((2, 2 * zc, 128), np.float32)
    for c in range(2):
        for at in range(128):
            rep[c, c * zc + at % zc, at] = 1.0

    vmem = pl.BlockSpec(memory_space=pltpu.VMEM)
    anywhere = pl.BlockSpec(memory_space=pl.ANY)
    dma = pltpu.SemaphoreType.DMA
    field, partner, alone, est = pl.pallas_call(
        functools.partial(kernel, spaces, samples),
        out_shape=(
            jax.ShapeDtypeStruct((pairs, slab * ny * nz // 128, 128), F32),
            jax.ShapeDtypeStruct((pairs, planes, cells), F32),
            jax.ShapeDtypeStruct((1, planes, cells), F32),
            jax.ShapeDtypeStruct((2,), F32),
        ),
        in_specs=[anywhere, vmem, pl.BlockSpec(memory_space=pltpu.SMEM)] + [vmem] * 6 + [
                  anywhere, anywhere, vmem, vmem, vmem],
        out_specs=(vmem, vmem, vmem, pl.BlockSpec(memory_space=pltpu.SMEM)),
        scratch_shapes=[
            pltpu.VMEM((pairs, 2, ny, nz), F32),
            pltpu.VMEM((2, pairs, 2, ny, nz), F32),
            pltpu.VMEM((2 * pairs, ky, nz), F32),
            pltpu.VMEM((2, spaces // 2, 2 * pairs, ky, nz), F32),
            pltpu.VMEM((spaces * ky, 2 * nz), F32),
            pltpu.VMEM((spaces, ky // 2, 4 * zc), F32),
            pltpu.VMEM((spaces, ky // 2, 4 * zc), F32),
            pltpu.VMEM(zt.shape, BF16),
            pltpu.VMEM(yt.shape, BF16),
            pltpu.VMEM((pairs, 2 * ny, nz), BF16),
            pltpu.VMEM((pairs, 2 * ny, nz), BF16),
            pltpu.VMEM((pairs, ny, nz), F32),
            pltpu.VMEM((4, ny, nz), F32),
            pltpu.VMEM((2, ny, nz), F32),
            pltpu.VMEM((4, ny, nz), F32),
            pltpu.VMEM((8, 128), F32),
            pltpu.VMEM((spaces, 8, 128), F32),
            pltpu.VMEM((8, 128), F32),
            pltpu.VMEM((samples, 8, 128), F32),
            dma((2, pairs, 2)), dma((2, pairs, 2)), dma, dma, dma,
            dma, dma((2, levels)), dma, dma((spaces // 2,)), dma,
            dma((spaces,)), dma((spaces,)), dma((spaces,)), dma((spaces,)),
            dma((samples,)), dma((samples,)),
        ],
        compiler_params=pltpu.CompilerParams(
            collective_id=0, has_side_effects=True, vmem_limit_bytes=60 * 1024 * 1024
        ),
    )(
        fine_state.astype(F32).reshape(pairs, slab, ny, nz),
        spectra, plane_assign, partner_state, coarse_state,
        turbine_x[None], turbine_y[None], turbine_z[None], thrust[None],
        jnp.asarray(zt), jnp.asarray(yt), jnp.asarray(zs), jnp.asarray(ys), jnp.asarray(rep),
    )
    field = field.reshape(pairs, ny * nz // 128, slab, 128).transpose(0, 2, 1, 3)
    return field.reshape(pairs, slab, ny * nz), partner, alone, est


def solution(mesh):
    return jax.shard_map(
        functools.partial(shards, mesh.shape["space"], mesh.shape["sample"]),
        mesh=mesh,
        in_specs=(
            P("sample", None, "space", None),
            P("sample", None),
            P("sample", "space", None),
            P("sample", None, None),
            P(("space", "sample"), None, None),
            P(),
            P(),
            P(),
            P(),
        ),
        out_specs=(
            P("sample", "space", None),
            P("sample", None, None),
            P(("space", "sample"), None, None),
            P(),
        ),
        check_vma=False,
    )
```
